512 devices in a mesh: pb: 16 (over x, y_lo), ka: 32 (over y_hi, z, core).
Axes of the slice: x: 4, y: 8 (y_hi: 2, y_lo: 4; y = y_hi * 4 + y_lo), z: 8, core: 2. Of those that a mesh axis runs over, the one named last changes fastest.
Arguments:
- tokens: bfloat16 [8192, 7168], P('ka', 'pb'), may hold values from -6 to 6
- kv_weight: bfloat16 [7168, 576], P('pb'), may hold values from -0.0625 to 0.0625
- queries: bfloat16 [8192, 36864], P('pb', 'ka'), may hold values from -384 to 384
- block_list: int32 [64, 16], P('pb'), may hold values from -1 to 63, as said below
Outputs:
- attended: bfloat16 [8192, 32768], P('pb', 'ka')
The draws below stay inside these ranges and needn't reach their ends.
Inputs may be any that keep to these rules, and one draw needn't show every extreme that they name: `block_list`: row i lists distinct key blocks j <= i in ascending order, followed by -1 in its unused slots; every row lists block 0; the row of the last block fills all 16 slots. The rows of one aligned group of 4 query blocks list at most 1 distinct blocks of one aligned group of 2 key blocks, and 1 is reached in every draw.
All inputs are finite; a program needn't handle non-finite values.
Results may differ from the reference program's by a relative error of at most 0.012.
Values may be sent and summed in bfloat16 or wider, within the bound.
A program may use at most 64 MiB of HBM per device.

```python
import math
import jax
import jax.numpy as jnp
from jax import lax

D = 7168
H = 64
KVL = 512
RD = 64
QK = 192
BLK = 128
MAXSEL = 16
KB = 2
NB = 64
QB = 4
CAP = 1
S = 8192
N_KA = 32


def draw_queries(key, part):
    values = jax.random.normal(jax.random.fold_in(key, 21), (S, H * (KVL + RD)), jnp.float32)
    values = jnp.clip(values, -6.0, 6.0)
    return values.astype(jnp.bfloat16)


def draw_block_list(key, part):
    set_scores = jax.random.randint(jax.random.fold_in(key, 31), (NB // QB, N_KA, KB), 0, 1 << 20)
    within = jnp.arange(KB, dtype=jnp.int32)
    set_scores = set_scores * KB + within
    anchor = (jnp.arange(N_KA, dtype=jnp.int32)[:, None] == 0) & (within[None, :] == 0)
    set_scores = jnp.where(anchor[None], jnp.int32(1 << 30), set_scores)
    beaten = jnp.sum((set_scores[..., None, :] > set_scores[..., :, None]).astype(jnp.int32), axis=-1)
    membership_flag = (beaten < CAP).reshape(NB // QB, NB)
    query_ids = jnp.arange(NB, dtype=jnp.int32)
    member_rows = membership_flag[query_ids // QB]
    candidate = member_rows & (query_ids[None, :] <= query_ids[:, None])
    priority = jax.random.randint(jax.random.fold_in(key, 32), (NB, NB), 0, 1 << 16) * NB + query_ids[None, :]
    last_row = query_ids[:, None] == NB - 1
    first_run = query_ids[None, :] < KB
    priority = priority + jnp.where(last_row & first_run, 1 << 29, 0) + jnp.where(query_ids[None, :] == 0, 1 << 30, 0)
    priority = jnp.where(candidate, priority, -1)
    ranked_blocks, picked = lax.top_k(priority, MAXSEL)
    wanted = jax.random.randint(jax.random.fold_in(key, 33), (NB, 1), 1, MAXSEL + 1)
    wanted = jnp.where(last_row, MAXSEL, wanted)
    valid = (ranked_blocks >= 0) & (jnp.arange(MAXSEL, dtype=jnp.int32)[None, :] < wanted)
    ordered = jnp.sort(jnp.where(valid, picked.astype(jnp.int32), NB), axis=1)
    return jnp.where(ordered == NB, -1, ordered).astype(jnp.int32)


def levels(key, extent, split, smallest, largest):
    def one(position, shards_of):
        steps = jax.random.uniform(jax.random.fold_in(jax.random.fold_in(key, 6), position), (shards_of,), jnp.float32, smallest / len(split), largest / len(split))
        return jnp.repeat(jnp.exp(steps), extent[position] // shards_of).reshape((-1,) + (1,) * (len(extent) - position - 1))

    level = one(*split[0])
    for cut in split[1:]:
        level = level * one(*cut)
    return level


def bell_draw(rng, shape, scale, bound, shards=(), held_as=jnp.bfloat16):
    level = levels(rng, shape, shards, -0.22, 0.18) if shards else 1.0
    drawn = jax.random.normal(rng, shape, jnp.float32) * scale * level
    return jnp.minimum(jnp.maximum(drawn, -bound), bound).astype(held_as)


def setup_inputs(seed: int = 0) -> dict:
    keys = jax.random.split(jax.random.key(seed), 5)
    return {
        "tokens": bell_draw(keys[0], (S, D), 1.0, 6.0, ((0, 32), (1, 16))),
        "kv_weight": bell_draw(keys[1], (D, KVL + RD), D ** -0.5, 0.0625, ((0, 16),)),
        "queries": draw_queries(jax.random.fold_in(keys[4], 71), 0),
        "block_list": draw_block_list(jax.random.fold_in(keys[4], 71), 0),
    }


def scale_rows(matrix):
    return matrix * lax.rsqrt(lax.optimization_barrier(jnp.mean(matrix * matrix, axis=-1, keepdims=True)) + 1e-06)

def rotate_cols(rotary, positions):
    half = rotary.shape[1] // 2
    steps = jnp.arange(half, dtype=jnp.float32)
    freq = jnp.exp(steps * (-2.0 * math.log(10000.0) / rotary.shape[1]))
    angle = positions.astype(jnp.float32)[:, None] * freq[None, :]
    cosine = jnp.cos(angle)
    sine = jnp.sin(angle)
    first = rotary[:, :half]
    second = rotary[:, half:]
    return jnp.concatenate([first * cosine - second * sine, second * cosine + first * sine], axis=1)

def reference(tokens, kv_weight, queries, block_list):
    width = KVL + RD
    projected = jnp.dot(tokens, kv_weight, preferred_element_type=jnp.float32)
    latent = scale_rows(projected[:, :KVL])
    rotary = rotate_cols(projected[:, KVL:], jnp.arange(S, dtype=jnp.int32))
    key_rows = jnp.concatenate([latent, rotary], axis=1).astype(jnp.bfloat16)
    key_blocks = key_rows.reshape(NB, BLK, width)
    query_blocks = queries.reshape(NB, BLK, H, width)
    offsets = jnp.arange(BLK, dtype=jnp.int32)
    factor = 1.0 / math.sqrt(QK)

    def one_block(inputs):
        block_index, query_block, listed = inputs
        chosen = jnp.maximum(listed, 0).astype(jnp.int32)
        selected_keys = key_blocks[chosen].reshape(MAXSEL * BLK, width).astype(jnp.float32)
        selected_values = selected_keys[:, :KVL]
        scores = jnp.einsum('qhd,kd->hqk', query_block.astype(jnp.float32), selected_keys) * factor
        key_pos = (chosen[:, None] * BLK + offsets[None, :]).reshape(MAXSEL * BLK)
        slot_live = jnp.broadcast_to((listed >= 0)[:, None], (MAXSEL, BLK)).reshape(MAXSEL * BLK)
        query_pos = block_index * BLK + offsets
        permitted_mask = slot_live[None, :] & (key_pos[None, :] <= query_pos[:, None])
        scores = jnp.where(permitted_mask[None], scores, -jnp.inf)
        highest = lax.optimization_barrier(jnp.max(scores, axis=-1, keepdims=True))
        weights = jnp.exp(scores - highest)
        weight_brain_float = (weights / lax.optimization_barrier(jnp.sum(weights, axis=-1, keepdims=True))).astype(jnp.bfloat16)
        blended = jnp.einsum('hqk,kd->qhd', weight_brain_float.astype(jnp.float32), selected_values)
        return blended.reshape(BLK, H * KVL).astype(jnp.bfloat16)
    result = lax.map(one_block, (jnp.arange(NB, dtype=jnp.int32), query_blocks, block_list))
    return result.reshape(NB * BLK, H * KVL)
```

```python
import functools
import math

import jax
import jax.numpy as jnp
from jax import lax
from jax.experimental import pallas as pl
from jax.experimental.pallas import tpu as pltpu
from jax.sharding import PartitionSpec as P

KVL = 512
RD = 64
WIDTH = KVL + RD
QK = 192
BLK = 128
QB = 4
HEADS = 2
YL = 4
NEG = -1e30
FAR = 1 << 20
F32 = jnp.float32
BF16 = jnp.bfloat16
I16 = jnp.int16
TOP = 32000.0


def div(a, n):
    return lax.div(a, jnp.int32(n))


def rem(a, n):
    return lax.rem(a, jnp.int32(n))


def kernel(
    n_pb, n_z,
    tok_hbm, w_hbm, bl_hbm, q_hbm,
    out_ref,
    tok_ref, w_ref, bl_ref, qv,
    lat_pool, rot_pool, guest_lat, guest_rot, rs_send, rs_recv, rx_send, rx_recv, ag_send, pieces, qs, acc, m_scr, l_scr, p_scr, f_scr, lim_scr,
    in_sem, rs_ss, rs_rs, rx_ss, rx_rs, ag_ss, ag_rs, start_ss, ring_ss, core_ss, pool_rs,
    far_in, gring_rs, gstart_ss, gring_ss, gout_ss,
):
    pb = lax.axis_index("pb")
    ka = lax.axis_index("ka")
    n_ka = 4 * n_z
    piece = BLK // n_pb
    events = 2 * n_z
    last_turn = n_z // 2 - 1
    y = div(ka, 2 * n_z)
    z = rem(div(ka, 2), n_z)
    c = rem(ka, 2)
    far = rem(ka + 2 * n_z, n_ka)
    twin = ka + 1 - 2 * c
    shift = n_pb - YL
    heavy = div(pb, shift)
    flip = y * (1 - heavy)
    own_pair = div(ka, 2)
    far_pair = div(far, 2)

    def beside(step):
        return y * 2 * n_z + rem(z + step + n_z, n_z) * 2 + c

    def send(src, dst, send_sem, recv_sem, to):
        return pltpu.make_async_remote_copy(
            src_ref=src, dst_ref=dst, send_sem=send_sem, recv_sem=recv_sem,
            device_id=to, device_id_type=pl.DeviceIdType.MESH,
        )

    barrier = pltpu.get_barrier_semaphore()

    def greet(to):
        pl.semaphore_signal(barrier, inc=1, device_id=to, device_id_type=pl.DeviceIdType.MESH)

    def greet_row(d, _):
        greet((rem(pb + d, n_pb), ka))
        return 0

    loads = [
        pltpu.make_async_copy(src, dst, in_sem.at[n])
        for n, (src, dst) in enumerate(
            [(tok_hbm, tok_ref), (w_hbm, w_ref), (bl_hbm, bl_ref), (q_hbm, qv)]
        )
    ]
    for load in loads:
        load.start()
    lax.fori_loop(1, n_pb, greet_row, 0)
    greet((pb, far))
    greet((pb, beside(1)))
    greet((pb, beside(-1)))
    greet((pb, twin))

    for load in loads[:3]:
        load.wait()
    part = lax.dot_general(
        tok_ref[...], w_ref[...], (((0,), (0,)), ((), ())), preferred_element_type=F32
    )
    listed = bl_ref[...]
    picks = jnp.where(listed == 2 * ka + 1, 1.0, 0.0)
    picked = jnp.max(jnp.max(picks, axis=1, keepdims=True), axis=0, keepdims=True)
    flag = jnp.broadcast_to(picked, (piece, 128))
    latents = part[:, :KVL]
    peak = jnp.maximum(jnp.max(jnp.abs(latents), axis=1, keepdims=True), 1e-30)
    coded = jnp.round(latents * (TOP / peak))
    unit = peak * (1.0 / TOP)
    for j in range(n_pb):
        low, high = [part[b * BLK + piece * j : b * BLK + piece * (j + 1)] for b in range(2)]
        both = [coded[b * BLK + piece * j : b * BLK + piece * (j + 1)] for b in range(2)]
        rs_send[j] = jnp.concatenate(both, axis=0).astype(jnp.int32).astype(I16)
        units = [unit[b * BLK + piece * j : b * BLK + piece * (j + 1)] for b in range(2)]
        units = jnp.concatenate([jnp.broadcast_to(u, (piece, RD)) for u in units], axis=1)
        tail = jnp.concatenate([low[:, KVL:], high[:, KVL:]], axis=1)
        rx_send[j] = jnp.concatenate([tail, jnp.where(flag > 0.5, -units, units)], axis=0)

    pl.semaphore_wait(barrier, n_pb + 3)
    pl.semaphore_signal(
        far_in, inc=1, device_id=(pb, far), device_id_type=pl.DeviceIdType.MESH
    )

    def rs_copy(to, slot):
        return send(rs_send.at[to], rs_recv.at[slot], rs_ss.at[to], rs_rs.at[slot], (to, ka))

    def rx_copy(to, slot):
        return send(rx_send.at[to], rx_recv.at[slot], rx_ss.at[to], rx_rs.at[slot], (to, ka))

    def start_rs(d, _):
        to = rem(pb + d, n_pb)
        rs_copy(to, pb).start()
        rx_copy(to, pb).start()
        return 0

    lax.fori_loop(1, n_pb, start_rs, 0)

    loads[3].wait()
    for i in range(QB):
        rows = slice(i * BLK, (i + 1) * BLK)
        for h in range(HEADS):
            mine = slice(h * BLK, (h + 1) * BLK)
            near = qv[rows, h * KVL : h * KVL + KVL + 128].astype(F32)[:, h * RD : h * RD + WIDTH]
            none = jnp.zeros((BLK, RD), F32)
            turn = near[:, KVL:]
            qs[i, mine, :KVL] = near[:, :KVL].astype(BF16)
            qs[i, mine, KVL:] = jnp.concatenate([turn, none, none, turn], axis=1).astype(BF16)
    m_scr[...] = jnp.full_like(m_scr, NEG)
    l_scr[...] = jnp.zeros_like(l_scr)
    acc[...] = jnp.zeros_like(acc)
    p_scr[...] = jnp.zeros_like(p_scr)
    f_scr[...] = jnp.ones_like(f_scr)

    def reach(slot, _):
        first = jnp.max(jnp.where(listed == 2 * slot, 1.0, 0.0), axis=1, keepdims=True)
        other = jnp.max(jnp.where(listed == 2 * slot + 1, 1.0, 0.0), axis=1, keepdims=True)
        block = QB * pb + lax.broadcasted_iota(jnp.int32, (QB, 1), 0)
        gap = (block - 2 * slot) * BLK
        limit = jnp.where(first > 0.5, gap, jnp.where(other > 0.5, gap - BLK, -FAR))
        lim_scr[slot] = jnp.broadcast_to(limit, (QB, HEADS * BLK))
        return 0

    lax.fori_loop(0, n_ka, reach, 0)

    row = lax.broadcasted_iota(jnp.int32, (2 * piece, RD), 0)
    col = lax.broadcasted_iota(jnp.int32, (2 * piece, RD), 1)
    place = ka * 2 * BLK + (row // piece) * BLK + pb * piece + row % piece
    freq = jnp.exp((col % (RD // 2)).astype(F32) * (-2.0 * math.log(10000.0) / RD))
    angle = place.astype(F32) * freq
    cosine = jnp.cos(angle)
    sine = jnp.where(col < RD // 2, -jnp.sin(angle), jnp.sin(angle))

    def take_rs(d, total):
        q = rem(pb + d, n_pb)
        rs_copy(q, q).wait_recv()
        rx_copy(q, q).wait_recv()
        return total[0] + decoded(rs_recv[q], rx_recv[q]), total[1] + rx_recv[q]

    def decoded(codes, extra):
        units = jnp.abs(extra[piece:])
        units = jnp.concatenate([units[:, :1], units[:, RD : RD + 1]], axis=0)
        return codes.astype(jnp.int32).astype(F32) * units

    rx_recv[pb] = rx_send[pb]
    start = (decoded(rs_send[pb], rx_send[pb]), rx_send[pb])
    latent, tail = lax.fori_loop(1, n_pb, take_rs, start)
    latent = latent * lax.rsqrt(jnp.mean(latent * latent, axis=-1, keepdims=True) + 1e-06)
    tail = tail[:piece]
    rotary = jnp.concatenate([tail[:, :RD], tail[:, RD:]], axis=0)
    turned = jnp.concatenate([rotary[:, RD // 2 :], rotary[:, : RD // 2]], axis=1)
    rotary = rotary * cosine + turned * sine
    keys = jnp.concatenate([latent, rotary], axis=1)

    for p in range(n_pb):
        second = rx_recv[p][piece : piece + 1, :1] < 0.0
        ag_send[p] = jnp.where(second, keys[piece:], keys[:piece]).astype(BF16)
    pieces[0, pb] = ag_send[pb]
    lends = (y == 1) & (c == 1)

    @pl.when(lends & (pb < YL))
    def _():
        pieces[2, pb] = ag_send[pb + shift]

    def piece_copy(part, slot, send_sem, src, to):
        return send(ag_send.at[src], pieces.at[part, slot], send_sem, ag_rs.at[part, slot], to)

    def each_ag(f, to, act):
        lent = jnp.where(lends & (to >= shift), 1, 0)
        dest = to - lent * shift
        part = f + lent * (2 - f)
        there = (dest, ka if f == 0 else far)
        away = (own_pair <= to) & (dest != pb) if f == 0 else own_pair <= to

        @pl.when(away)
        def _():
            act(piece_copy(part, pb, ag_ss.at[f, to], to, there))

    def take_piece(part, q):
        piece_copy(part, q, ag_ss.at[0, q], q, (q, ka)).wait_recv()

    def start_ag(f, d):
        each_ag(f, rem(pb + d, n_pb), lambda copy: copy.start())
        return 0

    lax.fori_loop(0, n_pb, lambda d, _: start_ag(0, d), 0)
    pl.semaphore_wait(far_in, 1)
    lax.fori_loop(0, n_pb, lambda d, _: start_ag(1, d), 0)

    class Both:
        def __init__(self, slot, sems, to, src=None, dst=None):
            src_refs, src_at = src or ((lat_pool, rot_pool), slot)
            dst_refs, arrived, dst_at = dst or ((lat_pool, rot_pool), pool_rs, slot)
            self.copies = [
                send(src_refs[n].at[src_at], dst_refs[n].at[dst_at], sems.at[n], arrived.at[n, dst_at], to)
                for n in range(2)
            ]

        def start(self):
            for copy in self.copies:
                copy.start()

        def wait_send(self):
            for copy in self.copies:
                copy.wait_send()

        def wait_recv(self):
            for copy in self.copies:
                copy.wait_recv()

    def core_copy(k, pair):
        return Both(2 * pair + c, core_ss.at[k], (pb, twin))

    def carried(pair):
        return (heavy == 1) & (c == 1) & (pair >= n_z)

    def own_opening(f, act):
        slot, pair = (ka, own_pair) if f == 0 else (far, far_pair)
        for side in range(2):
            act(Both(slot, start_ss.at[f, side], (pb, beside(1 - 2 * side))))
        act(core_copy(rem(f + heavy * y, 2), pair))

    def fill(refs, at, block):
        refs[0][at] = block[:, :KVL].astype(BF16)
        halves = [block[: BLK // 2, KVL:], block[BLK // 2 :, KVL:]]
        refs[1][at] = jnp.concatenate(halves, axis=1).astype(BF16)

    def open_ring(f):
        slot, pair = (ka, own_pair) if f == 0 else (far, far_pair)

        @pl.when((pair <= pb) & jnp.logical_not(carried(pair)))
        def _():
            def take(d, _):
                q = rem(pb + d, n_pb)
                take_piece(f, q)
                return 0

            lax.fori_loop(1 - f, n_pb, take, 0)
            fill((lat_pool, rot_pool), slot, pieces[f].astype(F32).reshape(BLK, WIDTH))
            own_opening(f, lambda copy: copy.start())

    open_ring(0)
    open_ring(1)

    guests = (guest_lat, guest_rot)
    host = (pb < YL) & (c == 1)

    def guest_start(side):
        to = (pb, beside(1 - 2 * side))
        return Both(z, gstart_ss.at[side], to, (guests, z), (guests, gring_rs, z))

    def guest_relay(at, side):
        to = (pb, beside(1 - 2 * side))
        return Both(at, gring_ss.at[at], to, (guests, at), (guests, gring_rs, at))

    def guest_out(at):
        slot = 2 * (n_z + at) + 1
        pools = (lat_pool, rot_pool)
        return Both(at, gout_ss.at[at], (pb + shift, ka), (guests, at), (pools, pool_rs, slot))

    def early_side(turn):
        return jnp.where(rem(z - 1 - turn + n_z, n_z) < rem(z + 1 + turn, n_z), 0, 1)

    def guest_event(e):
        turn = div(e, 2)
        final = div(e, n_z - 2)
        side = final + (1 - final) * rem(e, 2)
        at = rem(z - (1 + turn) * (1 - 2 * side) + n_z, n_z)
        onward = (turn < last_turn - 1) | ((turn == last_turn - 1) & (side == 1))
        return at, side, onward

    @pl.when(host)
    def _():
        @pl.when(n_z + z <= pb + shift)
        def _():
            def take(d, _):
                q = rem(pb + d, n_pb)

                @pl.when((d > 0) | (y == 0))
                def _():
                    take_piece(2, q)

                return 0

            lax.fori_loop(0, n_pb, take, 0)
            fill(guests, z, pieces[2].astype(F32).reshape(BLK, WIDTH))
            guest_start(0).start()
            guest_start(1).start()
            guest_out(z).start()

    def event(k):
        opening = 1 - div(k + events - 2, events)
        j = (k - 2) * (1 - opening)
        turn = div(j, 4)
        last = div(turn, last_turn)
        side = rem(j, 2)
        g = last * side + (1 - last) * rem(flip + div(j, 2), 2)
        at = rem(z - (1 + turn) * (1 - 2 * side) + n_z, n_z)
        pair = opening * (rem(flip + k, 2) * n_z + z) + (1 - opening) * (g * n_z + at)
        onward = (turn < last_turn - 1) | ((turn == last_turn - 1) & (g == side))
        lent = carried(pair)
        live = (pair <= pb) & ((k >= 2) | lent)
        return pair, side, onward & jnp.logical_not(lent), live

    def relay_copy(k, pair, side):
        return Both(2 * pair + c, ring_ss.at[k], (pb, beside(1 - 2 * side)))

    scale = math.log2(math.e) / math.sqrt(QK)
    shape = (BLK, HEADS * BLK)
    ahead = (
        lax.broadcasted_iota(jnp.int32, shape, 0) - lax.broadcasted_iota(jnp.int32, shape, 1) % BLK
    )

    def blend(i, values):
        return acc[i] * f_scr[i] + jnp.dot(values, p_scr[i], preferred_element_type=F32)

    def values_of(pair):
        return lat_pool[pl.ds(2 * pair, 2)].reshape(2 * BLK, KVL).T

    def attend(pair, before_pair):
        latents = lat_pool[pl.ds(2 * pair, 2)].reshape(2 * BLK, KVL)
        values = values_of(before_pair)
        none = jnp.zeros((BLK // 2, 128), BF16)
        parts = []
        for n in range(2):
            turn = rot_pool[2 * pair + n]
            parts += [jnp.concatenate([turn, none], 1), jnp.concatenate([none, turn], 1)]
        both = jnp.concatenate([latents, jnp.concatenate(parts, axis=0)], axis=1)
        limits = [lim_scr[2 * pair], lim_scr[2 * pair + 1]]

        def score(i):
            return lax.dot_general(
                both, qs[i], (((1,), (1,)), ((), ())), preferred_element_type=F32
            )

        scores = score(0)
        for i in range(QB):
            following = score(i + 1) if i + 1 < QB else None
            acc[i] = blend(i, values)
            seen = [
                jnp.where(ahead <= limits[n][i : i + 1], scores[n * BLK : (n + 1) * BLK], NEG)
                for n in range(2)
            ]
            scores = jnp.concatenate(seen, axis=0)
            before = m_scr[i]
            highest = jnp.maximum(before, jnp.max(scores, axis=0, keepdims=True))
            weights = jnp.exp2((scores - highest) * scale)
            fade = jnp.exp2((before - highest) * scale)
            l_scr[i] = l_scr[i] * fade + jnp.sum(weights, axis=0, keepdims=True)
            m_scr[i] = highest
            p_scr[i] = weights.astype(BF16)
            f_scr[i] = fade
            scores = following

    def drain_ring(k, _):
        pair, side, onward, live = event(k)

        @pl.when(live)
        def _():
            @pl.when(onward & (k >= 2))
            def _():
                relay_copy(k, pair, side).wait_send()

            core_copy(k, pair).wait_send()

        return 0

    def step(k, state):
        earlier, attended = state
        pair, side, onward, live = event(rem(k, events))

        @pl.when((k < events) & (k != events - 2) & live)
        def _():
            slot = 2 * pair + c
            Both(slot, core_ss.at[0], (pb, twin)).wait_recv()

            @pl.when(onward & (k >= 2))
            def _():
                relay_copy(k, pair, side).start()

            core_copy(k, pair).start()

        @pl.when(host & (k >= 1) & (k < n_z))
        def _():
            at, side, onward = guest_event(k - 1)

            @pl.when(n_z + at <= pb + shift)
            def _():
                guest_relay(at, side).wait_recv()

                @pl.when(onward)
                def _():
                    guest_relay(at, side).start()

                guest_out(at).start()


        ready = (k >= 1) & (earlier <= pb)

        @pl.when(ready)
        def _():
            Both(2 * earlier + 1 - c, core_ss.at[0], (pb, twin)).wait_recv()
            attend(earlier, jnp.where(attended < 0, earlier, attended))

        @pl.when(k == events - 2)
        def _():
            lax.fori_loop(0, events - 4, drain_ring, 0)

        @pl.when((k == events - 2) & live)
        def _():
            Both(2 * pair + c, core_ss.at[0], (pb, twin)).wait_recv()
            core_copy(k, pair).start()

        return pair, jnp.where(ready, earlier, attended)

    def drain_row(d, _):
        to = rem(pb + d, n_pb)

        @pl.when(d > 0)
        def _():
            rs_copy(to, pb).wait_send()
            rx_copy(to, pb).wait_send()

        each_ag(0, to, lambda copy: copy.wait_send())
        each_ag(1, to, lambda copy: copy.wait_send())
        return 0

    lax.fori_loop(0, n_pb, drain_row, 0)
    for f in range(2):
        pair = own_pair if f == 0 else far_pair

        @pl.when((pair <= pb) & jnp.logical_not(carried(pair)))
        def _():
            own_opening(f, lambda copy: copy.wait_send())

    _, attended = lax.fori_loop(0, events + 1, step, (jnp.int32(0), jnp.int32(-1)))

    values = values_of(attended)
    for i in range(QB):
        found = (blend(i, values) / l_scr[i]).astype(BF16)
        for h in range(HEADS):
            out_ref[i * BLK : (i + 1) * BLK, h * KVL : (h + 1) * KVL] = found[
                :, h * BLK : (h + 1) * BLK
            ].T

    lax.fori_loop(events - 4, events, drain_ring, 0)

    @pl.when(host)
    def _():
        @pl.when(n_z + z <= pb + shift)
        def _():
            guest_start(0).wait_send()
            guest_start(1).wait_send()
            guest_out(z).wait_send()

        def finish(e, _):
            at, side, onward = guest_event(e)

            @pl.when(n_z + at <= pb + shift)
            def _():
                @pl.when(onward)
                def _():
                    guest_relay(at, side).wait_send()

                guest_out(at).wait_send()

            return 0

        lax.fori_loop(0, n_z - 1, finish, 0)


def per_device(n_pb, n_z, tokens, kv_weight, queries, block_list):
    n_ka = 4 * n_z
    piece = BLK // n_pb
    rows = QB * BLK
    hbm = pl.BlockSpec(memory_space=pltpu.HBM)
    dma = pltpu.SemaphoreType.DMA
    return pl.pallas_call(
        functools.partial(kernel, n_pb, n_z),
        out_shape=jax.ShapeDtypeStruct((rows, HEADS * KVL), BF16),
        in_specs=[hbm, hbm, hbm, hbm],
        out_specs=pl.BlockSpec(memory_space=pltpu.VMEM),
        scratch_shapes=[
            pltpu.VMEM(tokens.shape[::-1], BF16),
            pltpu.VMEM(kv_weight.shape, BF16),
            pltpu.VMEM(block_list.shape, jnp.int32),
            pltpu.VMEM(queries.shape, BF16),
            pltpu.VMEM((n_ka, BLK, KVL), BF16),
            pltpu.VMEM((n_ka, BLK // 2, 2 * RD), BF16),
            pltpu.VMEM((n_z, BLK, KVL), BF16),
            pltpu.VMEM((n_z, BLK // 2, 2 * RD), BF16),
            pltpu.VMEM((n_pb, 2 * piece, KVL), I16),
            pltpu.VMEM((n_pb, 2 * piece, KVL), I16),
            pltpu.VMEM((n_pb, 2 * piece, 2 * RD), F32),
            pltpu.VMEM((n_pb, 2 * piece, 2 * RD), F32),
            pltpu.VMEM((n_pb, piece, WIDTH), BF16),
            pltpu.VMEM((3, n_pb, piece, WIDTH), BF16),
            pltpu.VMEM((QB, HEADS * BLK, KVL + 4 * RD), BF16),
            pltpu.VMEM((QB, KVL, HEADS * BLK), F32),
            pltpu.VMEM((QB, 1, HEADS * BLK), F32),
            pltpu.VMEM((QB, 1, HEADS * BLK), F32),
            pltpu.VMEM((QB, 2 * BLK, HEADS * BLK), BF16),
            pltpu.VMEM((QB, 1, HEADS * BLK), F32),
            pltpu.VMEM((n_ka, QB, HEADS * BLK), jnp.int32),
            dma((4,)),
            dma((n_pb,)),
            dma((n_pb,)),
            dma((n_pb,)),
            dma((n_pb,)),
            dma((2, n_pb)),
            dma((3, n_pb)),
            dma((2, 2, 2)),
            dma((2 * n_z, 2)),
            dma((2 * n_z, 2)),
            dma((2, n_ka)),
            pltpu.SemaphoreType.REGULAR,
            dma((2, n_z)),
            dma((2, 2)),
            dma((n_z, 2)),
            dma((n_z, 2)),
        ],
        compiler_params=pltpu.CompilerParams(
            collective_id=0, has_side_effects=True, vmem_limit_bytes=48 << 20
        ),
    )(*[pltpu.with_memory_space_constraint(a, pltpu.HBM) for a in (tokens.T, kv_weight, block_list, queries)])


def solution(mesh):
    n_pb, n_ka = mesh.shape["pb"], mesh.shape["ka"]
    return jax.shard_map(
        functools.partial(per_device, n_pb, n_ka // 4),
        mesh=mesh,
        in_specs=(P("ka", "pb"), P("pb", None), P("pb", "ka"), P("pb", None)),
        out_specs=P("pb", "ka"),
        check_vma=False,
    )
```

```python
import functools
import math

import jax
import jax.numpy as jnp
from jax import lax
from jax.experimental import pallas as pl
from jax.experimental.pallas import tpu as pltpu
from jax.sharding import PartitionSpec as P

KVL = 512
RD = 64
WIDTH = KVL + RD
QK = 192
BLK = 128
QB = 4
HEADS = 2
YL = 4
NEG = -1e30
FAR = 1 << 20
F32 = jnp.float32
BF16 = jnp.bfloat16


def div(a, n):
    return lax.div(a, jnp.int32(n))


def rem(a, n):
    return lax.rem(a, jnp.int32(n))


def kernel(
    n_pb, n_z,
    tok_hbm, w_hbm, bl_hbm, q_hbm,
    out_ref,
    tok_ref, w_ref, bl_ref, qv,
    lat_pool, rot_pool, guest_lat, guest_rot, rs_send, rs_recv, rx_send, rx_recv, ag_send, pieces, qs, acc, m_scr, l_scr, p_scr, f_scr, lim_scr,
    in_sem, rs_ss, rs_rs, rx_ss, rx_rs, ag_ss, ag_rs, start_ss, ring_ss, core_ss, pool_rs,
    far_in, gring_rs, gstart_ss, gring_ss, gout_ss,
):
    pb = lax.axis_index("pb")
    ka = lax.axis_index("ka")
    n_ka = 4 * n_z
    piece = BLK // n_pb
    events = 2 * n_z
    last_turn = n_z // 2 - 1
    y = div(ka, 2 * n_z)
    z = rem(div(ka, 2), n_z)
    c = rem(ka, 2)
    far = rem(ka + 2 * n_z, n_ka)
    twin = ka + 1 - 2 * c
    shift = n_pb - YL
    heavy = div(pb, shift)
    flip = y * (1 - heavy)
    own_pair = div(ka, 2)
    far_pair = div(far, 2)

    def beside(step):
        return y * 2 * n_z + rem(z + step + n_z, n_z) * 2 + c

    def send(src, dst, send_sem, recv_sem, to):
        return pltpu.make_async_remote_copy(
            src_ref=src, dst_ref=dst, send_sem=send_sem, recv_sem=recv_sem,
            device_id=to, device_id_type=pl.DeviceIdType.MESH,
        )

    barrier = pltpu.get_barrier_semaphore()

    def greet(to):
        pl.semaphore_signal(barrier, inc=1, device_id=to, device_id_type=pl.DeviceIdType.MESH)

    def greet_row(d, _):
        greet((rem(pb + d, n_pb), ka))
        return 0

    loads = [
        pltpu.make_async_copy(src, dst, in_sem.at[n])
        for n, (src, dst) in enumerate(
            [(tok_hbm, tok_ref), (w_hbm, w_ref), (bl_hbm, bl_ref), (q_hbm, qv)]
        )
    ]
    for load in loads:
        load.start()
    lax.fori_loop(1, n_pb, greet_row, 0)
    greet((pb, far))
    greet((pb, beside(1)))
    greet((pb, beside(-1)))
    greet((pb, twin))

    for load in loads[:3]:
        load.wait()
    part = lax.dot_general(
        tok_ref[...], w_ref[...], (((0,), (0,)), ((), ())), preferred_element_type=F32
    )
    listed = bl_ref[...]
    picks = jnp.where(listed == 2 * ka + 1, 1.0, 0.0)
    picked = jnp.max(jnp.max(picks, axis=1, keepdims=True), axis=0, keepdims=True)
    flag = jnp.broadcast_to(picked, (piece, 128))
    for j in range(n_pb):
        low, high = [part[b * BLK + piece * j : b * BLK + piece * (j + 1)] for b in range(2)]
        rs_send[j] = jnp.concatenate([low[:, :KVL], high[:, :KVL]], axis=0)
        tail = jnp.concatenate([low[:, KVL:], high[:, KVL:]], axis=1)
        rx_send[j] = jnp.concatenate([tail, flag], axis=0)

    pl.semaphore_wait(barrier, n_pb + 3)
    pl.semaphore_signal(
        far_in, inc=1, device_id=(pb, far), device_id_type=pl.DeviceIdType.MESH
    )

    def rs_copy(to, slot):
        return send(rs_send.at[to], rs_recv.at[slot], rs_ss.at[to], rs_rs.at[slot], (to, ka))

    def rx_copy(to, slot):
        return send(rx_send.at[to], rx_recv.at[slot], rx_ss.at[to], rx_rs.at[slot], (to, ka))

    def start_rs(d, _):
        to = rem(pb + d, n_pb)
        rs_copy(to, pb).start()
        rx_copy(to, pb).start()
        return 0

    lax.fori_loop(1, n_pb, start_rs, 0)

    loads[3].wait()
    for i in range(QB):
        rows = slice(i * BLK, (i + 1) * BLK)
        for h in range(HEADS):
            mine = slice(h * BLK, (h + 1) * BLK)
            near = qv[rows, h * KVL : h * KVL + KVL + 128].astype(F32)[:, h * RD : h * RD + WIDTH]
            none = jnp.zeros((BLK, RD), F32)
            turn = near[:, KVL:]
            qs[i, mine, :KVL] = near[:, :KVL].astype(BF16)
            qs[i, mine, KVL:] = jnp.concatenate([turn, none, none, turn], axis=1).astype(BF16)
    m_scr[...] = jnp.full_like(m_scr, NEG)
    l_scr[...] = jnp.zeros_like(l_scr)
    acc[...] = jnp.zeros_like(acc)
    p_scr[...] = jnp.zeros_like(p_scr)
    f_scr[...] = jnp.ones_like(f_scr)

    def reach(slot, _):
        first = jnp.max(jnp.where(listed == 2 * slot, 1.0, 0.0), axis=1, keepdims=True)
        other = jnp.max(jnp.where(listed == 2 * slot + 1, 1.0, 0.0), axis=1, keepdims=True)
        block = QB * pb + lax.broadcasted_iota(jnp.int32, (QB, 1), 0)
        gap = (block - 2 * slot) * BLK
        limit = jnp.where(first > 0.5, gap, jnp.where(other > 0.5, gap - BLK, -FAR))
        lim_scr[slot] = jnp.broadcast_to(limit, (QB, HEADS * BLK))
        return 0

    lax.fori_loop(0, n_ka, reach, 0)

    row = lax.broadcasted_iota(jnp.int32, (2 * piece, RD), 0)
    col = lax.broadcasted_iota(jnp.int32, (2 * piece, RD), 1)
    place = ka * 2 * BLK + (row // piece) * BLK + pb * piece + row % piece
    freq = jnp.exp((col % (RD // 2)).astype(F32) * (-2.0 * math.log(10000.0) / RD))
    angle = place.astype(F32) * freq
    cosine = jnp.cos(angle)
    sine = jnp.where(col < RD // 2, -jnp.sin(angle), jnp.sin(angle))

    def take_rs(d, total):
        q = rem(pb + d, n_pb)
        rs_copy(q, q).wait_recv()
        rx_copy(q, q).wait_recv()
        return total[0] + rs_recv[q], total[1] + rx_recv[q]

    rx_recv[pb] = rx_send[pb]
    start = (rs_send[pb], rx_send[pb])
    latent, tail = lax.fori_loop(1, n_pb, take_rs, start)
    latent = latent * lax.rsqrt(jnp.mean(latent * latent, axis=-1, keepdims=True) + 1e-06)
    tail = tail[:piece]
    rotary = jnp.concatenate([tail[:, :RD], tail[:, RD:]], axis=0)
    turned = jnp.concatenate([rotary[:, RD // 2 :], rotary[:, : RD // 2]], axis=1)
    rotary = rotary * cosine + turned * sine
    keys = jnp.concatenate([latent, rotary], axis=1)

    for p in range(n_pb):
        second = rx_recv[p][piece : piece + 1, :1] > 0.5
        ag_send[p] = jnp.where(second, keys[piece:], keys[:piece]).astype(BF16)
    pieces[0, pb] = ag_send[pb]
    lends = (y == 1) & (c == 1)

    @pl.when(lends & (pb < YL))
    def _():
        pieces[2, pb] = ag_send[pb + shift]

    def piece_copy(part, slot, send_sem, src, to):
        return send(ag_send.at[src], pieces.at[part, slot], send_sem, ag_rs.at[part, slot], to)

    def each_ag(f, to, act):
        lent = jnp.where(lends & (to >= shift), 1, 0)
        dest = to - lent * shift
        part = f + lent * (2 - f)
        there = (dest, ka if f == 0 else far)
        away = (own_pair <= to) & (dest != pb) if f == 0 else own_pair <= to

        @pl.when(away)
        def _():
            act(piece_copy(part, pb, ag_ss.at[f, to], to, there))

    def take_piece(part, q):
        piece_copy(part, q, ag_ss.at[0, q], q, (q, ka)).wait_recv()

    def start_ag(f, d):
        each_ag(f, rem(pb + d, n_pb), lambda copy: copy.start())
        return 0

    lax.fori_loop(0, n_pb, lambda d, _: start_ag(0, d), 0)
    pl.semaphore_wait(far_in, 1)
    lax.fori_loop(0, n_pb, lambda d, _: start_ag(1, d), 0)

    class Both:
        def __init__(self, slot, sems, to, src=None, dst=None):
            src_refs, src_at = src or ((lat_pool, rot_pool), slot)
            dst_refs, arrived, dst_at = dst or ((lat_pool, rot_pool), pool_rs, slot)
            self.copies = [
                send(src_refs[n].at[src_at], dst_refs[n].at[dst_at], sems.at[n], arrived.at[n, dst_at], to)
                for n in range(2)
            ]

        def start(self):
            for copy in self.copies:
                copy.start()

        def wait_send(self):
            for copy in self.copies:
                copy.wait_send()

        def wait_recv(self):
            for copy in self.copies:
                copy.wait_recv()

    def core_copy(k, pair):
        return Both(2 * pair + c, core_ss.at[k], (pb, twin))

    def carried(pair):
        return (heavy == 1) & (c == 1) & (pair >= n_z)

    def own_opening(f, act):
        slot, pair = (ka, own_pair) if f == 0 else (far, far_pair)
        for side in range(2):
            act(Both(slot, start_ss.at[f, side], (pb, beside(1 - 2 * side))))
        act(core_copy(rem(f + heavy * y, 2), pair))

    def fill(refs, at, block):
        refs[0][at] = block[:, :KVL].astype(BF16)
        halves = [block[: BLK // 2, KVL:], block[BLK // 2 :, KVL:]]
        refs[1][at] = jnp.concatenate(halves, axis=1).astype(BF16)

    def open_ring(f):
        slot, pair = (ka, own_pair) if f == 0 else (far, far_pair)

        @pl.when((pair <= pb) & jnp.logical_not(carried(pair)))
        def _():
            def take(d, _):
                q = rem(pb + d, n_pb)
                take_piece(f, q)
                return 0

            lax.fori_loop(1 - f, n_pb, take, 0)
            fill((lat_pool, rot_pool), slot, pieces[f].astype(F32).reshape(BLK, WIDTH))
            own_opening(f, lambda copy: copy.start())

    open_ring(0)
    open_ring(1)

    guests = (guest_lat, guest_rot)
    host = (pb < YL) & (c == 1)

    def guest_start(side):
        to = (pb, beside(1 - 2 * side))
        return Both(z, gstart_ss.at[side], to, (guests, z), (guests, gring_rs, z))

    def guest_relay(at, side):
        to = (pb, beside(1 - 2 * side))
        return Both(at, gring_ss.at[at], to, (guests, at), (guests, gring_rs, at))

    def guest_out(at):
        slot = 2 * (n_z + at) + 1
        pools = (lat_pool, rot_pool)
        return Both(at, gout_ss.at[at], (pb + shift, ka), (guests, at), (pools, pool_rs, slot))

    def early_side(turn):
        return jnp.where(rem(z - 1 - turn + n_z, n_z) < rem(z + 1 + turn, n_z), 0, 1)

    def guest_event(e):
        turn = div(e, 2)
        final = div(e, n_z - 2)
        side = final + (1 - final) * rem(e, 2)
        at = rem(z - (1 + turn) * (1 - 2 * side) + n_z, n_z)
        onward = (turn < last_turn - 1) | ((turn == last_turn - 1) & (side == 1))
        return at, side, onward

    @pl.when(host)
    def _():
        @pl.when(n_z + z <= pb + shift)
        def _():
            def take(d, _):
                q = rem(pb + d, n_pb)

                @pl.when((d > 0) | (y == 0))
                def _():
                    take_piece(2, q)

                return 0

            lax.fori_loop(0, n_pb, take, 0)
            fill(guests, z, pieces[2].astype(F32).reshape(BLK, WIDTH))
            guest_start(0).start()
            guest_start(1).start()
            guest_out(z).start()

    def event(k):
        opening = 1 - div(k + events - 2, events)
        j = (k - 2) * (1 - opening)
        turn = div(j, 4)
        last = div(turn, last_turn)
        side = rem(j, 2)
        g = last * side + (1 - last) * rem(flip + div(j, 2), 2)
        at = rem(z - (1 + turn) * (1 - 2 * side) + n_z, n_z)
        pair = opening * (rem(flip + k, 2) * n_z + z) + (1 - opening) * (g * n_z + at)
        onward = (turn < last_turn - 1) | ((turn == last_turn - 1) & (g == side))
        lent = carried(pair)
        live = (pair <= pb) & ((k >= 2) | lent)
        return pair, side, onward & jnp.logical_not(lent), live

    def relay_copy(k, pair, side):
        return Both(2 * pair + c, ring_ss.at[k], (pb, beside(1 - 2 * side)))

    scale = math.log2(math.e) / math.sqrt(QK)
    shape = (BLK, HEADS * BLK)
    ahead = (
        lax.broadcasted_iota(jnp.int32, shape, 0) - lax.broadcasted_iota(jnp.int32, shape, 1) % BLK
    )

    def blend(i, values):
        return acc[i] * f_scr[i] + jnp.dot(values, p_scr[i], preferred_element_type=F32)

    def values_of(pair):
        return lat_pool[pl.ds(2 * pair, 2)].reshape(2 * BLK, KVL).T

    def attend(pair, before_pair):
        latents = lat_pool[pl.ds(2 * pair, 2)].reshape(2 * BLK, KVL)
        values = values_of(before_pair)
        none = jnp.zeros((BLK // 2, 128), BF16)
        parts = []
        for n in range(2):
            turn = rot_pool[2 * pair + n]
            parts += [jnp.concatenate([turn, none], 1), jnp.concatenate([none, turn], 1)]
        both = jnp.concatenate([latents, jnp.concatenate(parts, axis=0)], axis=1)
        limits = [lim_scr[2 * pair], lim_scr[2 * pair + 1]]

        def score(i):
            return lax.dot_general(
                both, qs[i], (((1,), (1,)), ((), ())), preferred_element_type=F32
            )

        scores = score(0)
        for i in range(QB):
            following = score(i + 1) if i + 1 < QB else None
            acc[i] = blend(i, values)
            seen = [
                jnp.where(ahead <= limits[n][i : i + 1], scores[n * BLK : (n + 1) * BLK], NEG)
                for n in range(2)
            ]
            scores = jnp.concatenate(seen, axis=0)
            before = m_scr[i]
            highest = jnp.maximum(before, jnp.max(scores, axis=0, keepdims=True))
            weights = jnp.exp2((scores - highest) * scale)
            fade = jnp.exp2((before - highest) * scale)
            l_scr[i] = l_scr[i] * fade + jnp.sum(weights, axis=0, keepdims=True)
            m_scr[i] = highest
            p_scr[i] = weights.astype(BF16)
            f_scr[i] = fade
            scores = following

    def drain_ring(k, _):
        pair, side, onward, live = event(k)

        @pl.when(live)
        def _():
            @pl.when(onward & (k >= 2))
            def _():
                relay_copy(k, pair, side).wait_send()

            core_copy(k, pair).wait_send()

        return 0

    def step(k, state):
        earlier, attended = state
        pair, side, onward, live = event(rem(k, events))

        @pl.when((k < events) & (k != events - 2) & live)
        def _():
            slot = 2 * pair + c
            Both(slot, core_ss.at[0], (pb, twin)).wait_recv()

            @pl.when(onward & (k >= 2))
            def _():
                relay_copy(k, pair, side).start()

            core_copy(k, pair).start()

        @pl.when(host & (k >= 1) & (k < n_z))
        def _():
            at, side, onward = guest_event(k - 1)

            @pl.when(n_z + at <= pb + shift)
            def _():
                guest_relay(at, side).wait_recv()

                @pl.when(onward)
                def _():
                    guest_relay(at, side).start()

                guest_out(at).start()


        ready = (k >= 1) & (earlier <= pb)

        @pl.when(ready)
        def _():
            Both(2 * earlier + 1 - c, core_ss.at[0], (pb, twin)).wait_recv()
            attend(earlier, jnp.where(attended < 0, earlier, attended))

        @pl.when(k == events - 2)
        def _():
            lax.fori_loop(0, events - 4, drain_ring, 0)

        @pl.when((k == events - 2) & live)
        def _():
            Both(2 * pair + c, core_ss.at[0], (pb, twin)).wait_recv()
            core_copy(k, pair).start()

        return pair, jnp.where(ready, earlier, attended)

    def drain_row(d, _):
        to = rem(pb + d, n_pb)

        @pl.when(d > 0)
        def _():
            rs_copy(to, pb).wait_send()
            rx_copy(to, pb).wait_send()

        each_ag(0, to, lambda copy: copy.wait_send())
        each_ag(1, to, lambda copy: copy.wait_send())
        return 0

    lax.fori_loop(0, n_pb, drain_row, 0)
    for f in range(2):
        pair = own_pair if f == 0 else far_pair

        @pl.when((pair <= pb) & jnp.logical_not(carried(pair)))
        def _():
            own_opening(f, lambda copy: copy.wait_send())

    _, attended = lax.fori_loop(0, events + 1, step, (jnp.int32(0), jnp.int32(-1)))

    values = values_of(attended)
    for i in range(QB):
        found = (blend(i, values) / l_scr[i]).astype(BF16)
        for h in range(HEADS):
            out_ref[i * BLK : (i + 1) * BLK, h * KVL : (h + 1) * KVL] = found[
                :, h * BLK : (h + 1) * BLK
            ].T

    lax.fori_loop(events - 4, events, drain_ring, 0)

    @pl.when(host)
    def _():
        @pl.when(n_z + z <= pb + shift)
        def _():
            guest_start(0).wait_send()
            guest_start(1).wait_send()
            guest_out(z).wait_send()

        def finish(e, _):
            at, side, onward = guest_event(e)

            @pl.when(n_z + at <= pb + shift)
            def _():
                @pl.when(onward)
                def _():
                    guest_relay(at, side).wait_send()

                guest_out(at).wait_send()

            return 0

        lax.fori_loop(0, n_z - 1, finish, 0)


def per_device(n_pb, n_z, tokens, kv_weight, queries, block_list):
    n_ka = 4 * n_z
    piece = BLK // n_pb
    rows = QB * BLK
    hbm = pl.BlockSpec(memory_space=pltpu.HBM)
    dma = pltpu.SemaphoreType.DMA
    return pl.pallas_call(
        functools.partial(kernel, n_pb, n_z),
        out_shape=jax.ShapeDtypeStruct((rows, HEADS * KVL), BF16),
        in_specs=[hbm, hbm, hbm, hbm],
        out_specs=pl.BlockSpec(memory_space=pltpu.VMEM),
        scratch_shapes=[
            pltpu.VMEM(tokens.shape[::-1], BF16),
            pltpu.VMEM(kv_weight.shape, BF16),
            pltpu.VMEM(block_list.shape, jnp.int32),
            pltpu.VMEM(queries.shape, BF16),
            pltpu.VMEM((n_ka, BLK, KVL), BF16),
            pltpu.VMEM((n_ka, BLK // 2, 2 * RD), BF16),
            pltpu.VMEM((n_z, BLK, KVL), BF16),
            pltpu.VMEM((n_z, BLK // 2, 2 * RD), BF16),
            pltpu.VMEM((n_pb, 2 * piece, KVL), F32),
            pltpu.VMEM((n_pb, 2 * piece, KVL), F32),
            pltpu.VMEM((n_pb, 2 * piece, 2 * RD), F32),
            pltpu.VMEM((n_pb, 2 * piece, 2 * RD), F32),
            pltpu.VMEM((n_pb, piece, WIDTH), BF16),
            pltpu.VMEM((3, n_pb, piece, WIDTH), BF16),
            pltpu.VMEM((QB, HEADS * BLK, KVL + 4 * RD), BF16),
            pltpu.VMEM((QB, KVL, HEADS * BLK), F32),
            pltpu.VMEM((QB, 1, HEADS * BLK), F32),
            pltpu.VMEM((QB, 1, HEADS * BLK), F32),
            pltpu.VMEM((QB, 2 * BLK, HEADS * BLK), BF16),
            pltpu.VMEM((QB, 1, HEADS * BLK), F32),
            pltpu.VMEM((n_ka, QB, HEADS * BLK), jnp.int32),
            dma((4,)),
            dma((n_pb,)),
            dma((n_pb,)),
            dma((n_pb,)),
            dma((n_pb,)),
            dma((2, n_pb)),
            dma((3, n_pb)),
            dma((2, 2, 2)),
            dma((2 * n_z, 2)),
            dma((2 * n_z, 2)),
            dma((2, n_ka)),
            pltpu.SemaphoreType.REGULAR,
            dma((2, n_z)),
            dma((2, 2)),
            dma((n_z, 2)),
            dma((n_z, 2)),
        ],
        compiler_params=pltpu.CompilerParams(
            collective_id=0, has_side_effects=True, vmem_limit_bytes=48 << 20
        ),
    )(*[pltpu.with_memory_space_constraint(a, pltpu.HBM) for a in (tokens.T, kv_weight, block_list, queries)])


def solution(mesh):
    n_pb, n_ka = mesh.shape["pb"], mesh.shape["ka"]
    return jax.shard_map(
        functools.partial(per_device, n_pb, n_ka // 4),
        mesh=mesh,
        in_specs=(P("ka", "pb"), P("pb", None), P("pb", "ka"), P("pb", None)),
        out_specs=P("pb", "ka"),
        check_vma=False,
    )
```
